512 devices in a mesh: wide: 64 (over y, z_lo, core), narrow: 8 (over z_hi, x).
Axes of the slice: x: 4, y: 8, z: 8 (z_hi: 2, z_lo: 4; z = z_hi * 4 + z_lo), core: 2. Of those that a mesh axis runs over, the one named last changes fastest.
Arguments:
- integrals: bfloat16 [2048, 256, 256], P('narrow', 'wide'), may hold values from -6 to 6
- fitted: bfloat16 [2048, 256, 256], P('narrow', 'wide'), may hold values from -0.00390625 to 0.00390625
- occupied: bfloat16 [256, 1024], P('wide'), may hold values from -0.375 to 0.375
- pattern: int32 [8, 8], replicated, may hold values 0 or 1
Outputs:
- exchange_matrix: float32 [256, 256], P('wide')
The draws below stay inside these ranges and needn't reach their ends.
All inputs are finite; a program needn't handle non-finite values.
Results may differ from the reference program's by a relative error of at most 0.0018.
Values may be sent and summed in bfloat16 or wider, within the bound.
A program may use at most 64 MiB of HBM per device.

```python
import jax
import jax.numpy as jnp
from jax import lax

Q = 2048
OCC = 1024
NBLK = 8
NB = 256


def set_ends(entries, stream_key, low, largest):
    extent = entries.shape
    spot = [jax.random.randint(jax.random.fold_in(stream_key, axis), (), 0, extent[axis]) for axis in range(len(extent))]
    entries = entries.at[tuple(spot)].set(low)
    longest = extent.index(max(extent))
    spot[longest] = (spot[longest] + 1) % extent[longest]
    return entries.at[tuple(spot)].set(largest)


def block_levels(stream_key, extent, pieces, least, top_value):
    loudness = 1.0
    for dim, parts in pieces:
        heights = jax.random.uniform(jax.random.fold_in(jax.random.fold_in(stream_key, 6), dim), (parts,), jnp.float32, least / len(pieces), top_value / len(pieces))
        loudness = loudness * jnp.repeat(jnp.exp(heights), extent[dim] // parts).reshape((-1,) + (1,) * (len(extent) - 1 - dim))
    return loudness


def normal_values(key, shape, width, most, pieces=(), kind=jnp.bfloat16):
    entries = jax.random.normal(key, shape, jnp.float32) * width
    if len(pieces) > 0:
        entries = block_levels(key, shape, pieces, -0.22, 0.18) * entries
    return jnp.clip(entries, min=-most, max=most).astype(kind)


def setup_inputs(seed: int = 0) -> dict:
    keys = jax.random.split(jax.random.key(seed), 5)
    return {
        "integrals": normal_values(keys[0], (Q, NB, NB), 1.0, 6.0, ((0, 8), (1, 64))),
        "fitted": normal_values(keys[1], (Q, NB, NB), (Q * OCC) ** -0.5, 0.00390625, ((0, 8), (1, 64))),
        "occupied": normal_values(keys[2], (NB, OCC), NB ** -0.5, 0.375, ((0, 64),)),
        "pattern": set_ends((jax.random.randint(keys[3], (NBLK, NBLK), 0, 2) < 1).astype(jnp.int32), jax.random.fold_in(keys[3], 1), 0, 1),
    }


def reference(integrals, fitted, occupied, pattern):
    basis = integrals.shape[1]
    block_width = basis // NBLK
    block_ids = jnp.arange(basis) // block_width
    live = pattern[block_ids[:, None], block_ids[None, :]]
    live_mask = live.astype(jnp.float32)
    full_panel = occupied.astype(jnp.float32)
    aux_step = min(64, Q)
    ints_blocks = integrals.reshape(Q // aux_step, aux_step, basis, basis)
    fitted_blocks = fitted.reshape(Q // aux_step, aux_step, basis, basis)

    def accumulate(carry, blocks_pair):
        ints_part, fitted_part = blocks_pair
        half_ints = jnp.einsum("qml,li->qmi", ints_part.astype(jnp.float32) * live_mask, full_panel,
                               precision=lax.Precision.HIGHEST).astype(jnp.bfloat16)
        half_fitted = jnp.einsum("qml,li->qmi", fitted_part.astype(jnp.float32) * live_mask, full_panel,
                                 precision=lax.Precision.HIGHEST).astype(jnp.bfloat16)
        carry = carry + jnp.einsum("qmi,qni->mn", half_ints.astype(jnp.float32), half_fitted.astype(jnp.float32),
                                   precision=lax.Precision.HIGHEST)
        return carry, None

    partial_value, _ = lax.scan(accumulate, jnp.zeros((basis, basis), jnp.float32), (ints_blocks, fitted_blocks))
    return partial_value + partial_value.T
```

```python
import functools

import jax
import jax.numpy as jnp
from jax import lax
from jax.experimental import pallas as pl
from jax.experimental.pallas import tpu as pltpu
from jax.sharding import PartitionSpec as P

NBLK = 8
NY, NZ, NC, NH, NX = 8, 4, 2, 2, 4
Y_ORDER = (4, 1, 7, 2, 6, 3, 5, 0)


def mm_nt(a, b):
    return lax.dot_general(a, b, (((1,), (1,)), ((), ())), preferred_element_type=jnp.float32)


def mm(a, b):
    return lax.dot_general(a, b, (((1,), (0,)), ((), ())), preferred_element_type=jnp.float32)


def split(v):
    hi = v.astype(jnp.bfloat16)
    return hi, (v - hi.astype(jnp.float32)).astype(jnp.bfloat16)


def kernel(ints, fit, occ, pat, out, r_int, r_fit, c_own, c_all, mask, th, tl, s_all, r_a, s_b, r_b,
           send_sem, int_sem, fit_sem, own_sem, all_sem, a_sem, b_sem, send2_sem, senda_sem, sendb_sem):
    w = lax.axis_index("wide")
    n = lax.axis_index("narrow")
    y = w // (NZ * NC)
    zc = w % (NZ * NC)
    z = zc // NC
    c = zc % NC
    h = n // NX
    x = n % NX
    nw = NY * NZ * NC
    nq = ints.shape[0] // nw
    rows = ints.shape[1]
    basis = ints.shape[2]
    lanes = c_own.shape[2]

    def wide_id(yy, zz, cc):
        return (yy * NZ + zz) * NC + cc

    barrier = pltpu.get_barrier_semaphore()

    def greet(ww, nn):
        pl.semaphore_signal(barrier, inc=1, device_id={"wide": ww, "narrow": nn})

    def plane(o, carry):
        for dy in Y_ORDER:
            p = lax.rem(y + dy, NY) * (NZ * NC) + (zc ^ o)
            if dy == 0:
                @pl.when(o != 0)
                def _():
                    greet(p, n)
            else:
                greet(p, n)
        return carry

    lax.fori_loop(0, NZ * NC, plane, 0)

    for j in range(1, NH * NX):
        nn = lax.rem(n + j, NH * NX)
        for dz in range(NZ):
            greet(wide_id(y, z ^ dz, c), nn)
    for dx in range(1, NX):
        greet(wide_id(y, z, 1 - c), h * NX + lax.rem(x + dx, NX))
    peers = nw - 1 + (NH * NX - 1) * NZ + NX - 1

    lane = lax.broadcasted_iota(jnp.int32, (1, basis), 1) // (basis // NBLK)
    for a in range(NBLK):
        v = jnp.zeros((1, basis), jnp.float32)
        for b in range(NBLK):
            v = jnp.where(lane == b, pat[a, b].astype(jnp.float32), v)
        mask[pl.ds(a * (basis // NBLK), basis // NBLK), :] = jnp.broadcast_to(
            v, (basis // NBLK, basis)).astype(jnp.bfloat16)

    pl.semaphore_wait(barrier, peers)

    def panel_copy(p, k):
        return pltpu.make_async_remote_copy(
            src_ref=occ.at[:, pl.ds(pl.multiple_of(k * lanes, lanes), lanes)], dst_ref=c_own.at[w],
            send_sem=send2_sem, recv_sem=own_sem, device_id={"wide": p, "narrow": n})

    def row_copy(src, dst, sem, p):
        return pltpu.make_async_remote_copy(
            src_ref=src.at[pl.ds(p * nq, nq)], dst_ref=dst.at[:, w],
            send_sem=send_sem, recv_sem=sem, device_id={"wide": p, "narrow": n})

    def everyone(start):
        def step(o, carry):
            for dy in Y_ORDER:
                p = lax.rem(y + dy, NY) * (NZ * NC) + (zc ^ o)
                if dy == 0:
                    @pl.when(o != 0)
                    def _():
                        start(p)
                else:
                    start(p)
            return carry
        lax.fori_loop(0, NZ * NC, step, 0)

    everyone(lambda p: panel_copy(p, x * NC + p % NC).start())
    pltpu.make_async_copy(occ.at[:, pl.ds(pl.multiple_of((x * NC + c) * lanes, lanes), lanes)], c_own.at[w], own_sem).start()
    everyone(lambda p: row_copy(ints, r_int, int_sem, p).start())
    pltpu.make_async_copy(ints.at[pl.ds(w * nq, nq)], r_int.at[:, w], int_sem).start()
    everyone(lambda p: row_copy(fit, r_fit, fit_sem, p).start())
    pltpu.make_async_copy(fit.at[pl.ds(w * nq, nq)], r_fit.at[:, w], fit_sem).start()

    pltpu.make_async_copy(c_own, c_own, own_sem).wait()
    k_own = x * NC + c

    def pass_on(dx, dc):
        return pltpu.make_async_remote_copy(
            src_ref=c_own, dst_ref=c_all.at[k_own], send_sem=send2_sem, recv_sem=all_sem,
            device_id={"wide": wide_id(y, z, c ^ dc), "narrow": h * NX + lax.rem(x + dx, NX)})

    others = [(dx, dc) for dx in range(NX) for dc in range(NC) if (dx, dc) != (0, 0)]
    for dx, dc in others:
        pass_on(dx, dc).start()
    pltpu.make_async_copy(c_own, c_all.at[k_own], all_sem).start()
    pltpu.make_async_copy(c_all, c_all, all_sem).wait()
    panel = jnp.concatenate([c_all[k].reshape(basis, lanes) for k in range(NX * NC)], axis=1)
    p_hi, p_lo = split(mm_nt(panel, panel))

    pltpu.make_async_copy(r_int, r_int, int_sem).wait()
    keep = mask[...]
    for q in range(nq):
        a = r_int[q].reshape(basis, basis) * keep
        hi, lo = split(mm(a, p_hi) + mm(a, p_lo))
        th[q] = hi
        tl[q] = lo

    pltpu.make_async_copy(r_fit, r_fit, fit_sem).wait()
    m = jnp.zeros((basis, basis), jnp.float32)
    for q in range(nq):
        f = r_fit[q].reshape(basis, basis) * keep
        m = m + mm_nt(th[q], f) + mm_nt(tl[q], f)
    s_all[...] = (m + m.T).reshape(NY, NZ, NC, rows, basis)

    me_a = y * NC + c

    def copy_a(dy, dc):
        yy = lax.rem(y + dy, NY)
        cc = c ^ dc
        return pltpu.make_async_remote_copy(
            src_ref=s_all.at[yy, :, cc], dst_ref=r_a.at[me_a], send_sem=senda_sem, recv_sem=a_sem,
            device_id={"wide": wide_id(yy, z, cc), "narrow": n})

    for dy in Y_ORDER:
        for dc in range(NC):
            if (dy, dc) != (0, 0):
                copy_a(dy, dc).start()
    pltpu.make_async_copy(s_all.at[y, :, c], r_a.at[me_a], a_sem).start()
    pltpu.make_async_copy(r_a, r_a, a_sem).wait()
    s_b[...] = jnp.sum(r_a[...], axis=0)

    me_b = n * NZ + z

    def copy_b(j, dz):
        nn = lax.rem(n + j, NH * NX)
        zz = z ^ dz
        return pltpu.make_async_remote_copy(
            src_ref=s_b.at[zz], dst_ref=r_b.at[me_b], send_sem=sendb_sem, recv_sem=b_sem,
            device_id={"wide": wide_id(y, zz, c), "narrow": nn})

    for j in range(NH * NX):
        for dz in range(NZ):
            if (j, dz) != (0, 0):
                copy_b(j, dz).start()
    pltpu.make_async_copy(s_b.at[z], r_b.at[me_b], b_sem).start()
    pltpu.make_async_copy(r_b, r_b, b_sem).wait()
    out[...] = jnp.sum(r_b[...], axis=0)

    sent = ints.at[pl.ds(0, (nw - 1) * nq)]
    pltpu.make_async_copy(sent, sent, send_sem).wait()
    pltpu.make_async_copy(sent, sent, send_sem).wait()
    own = c_own.at[pl.ds(0, nw - 1)]
    pltpu.make_async_copy(own, own, send2_sem).wait()
    rest = c_all.at[pl.ds(0, NX * NC - 1)]
    pltpu.make_async_copy(rest, rest, send2_sem).wait()
    ra = r_a.at[pl.ds(0, NY * NC - 1)]
    pltpu.make_async_copy(ra, ra, senda_sem).wait()
    rb = r_b.at[pl.ds(0, NH * NX * NZ - 1)]
    pltpu.make_async_copy(rb, rb, sendb_sem).wait()


def on_device(integrals, fitted, occupied, pattern):
    aux, rows, basis = integrals.shape
    width = occupied.shape[1]
    nw = NY * NZ * NC
    nq = aux // nw
    lanes = width // (NX * NC)
    bf, f32 = jnp.bfloat16, jnp.float32
    any_space = pl.BlockSpec(memory_space=pl.ANY)
    dma = pltpu.SemaphoreType.DMA
    return pl.pallas_call(
        kernel,
        out_shape=jax.ShapeDtypeStruct((rows, basis), f32),
        in_specs=[any_space, any_space, any_space, pl.BlockSpec(memory_space=pltpu.SMEM)],
        out_specs=pl.BlockSpec(memory_space=pltpu.VMEM),
        scratch_shapes=[
            pltpu.VMEM((nq, nw, rows, basis), bf),
            pltpu.VMEM((nq, nw, rows, basis), bf),
            pltpu.VMEM((nw, rows, lanes), bf),
            pltpu.VMEM((NX * NC, nw, rows, lanes), bf),
            pltpu.VMEM((basis, basis), bf),
            pltpu.VMEM((nq, basis, basis), bf),
            pltpu.VMEM((nq, basis, basis), bf),
            pltpu.VMEM((NY, NZ, NC, rows, basis), f32),
            pltpu.VMEM((NY * NC, NZ, rows, basis), f32),
            pltpu.VMEM((NZ, rows, basis), f32),
            pltpu.VMEM((NH * NX * NZ, rows, basis), f32),
        ] + [dma] * 10,
        compiler_params=pltpu.CompilerParams(collective_id=0, has_side_effects=True),
    )(integrals, fitted, occupied, pattern)


def solution(mesh):
    in_specs = (P("narrow", "wide", None), P("narrow", "wide", None), P("wide", None), P())
    out_specs = P("wide", None)
    return jax.shard_map(
        on_device, mesh=mesh, in_specs=in_specs, out_specs=out_specs, check_vma=False
    )
```

```python
import functools

import jax
import jax.numpy as jnp
from jax import lax
from jax.experimental import pallas as pl
from jax.experimental.pallas import tpu as pltpu
from jax.sharding import PartitionSpec as P

NBLK = 8
NY, NZ, NC, NH, NX = 8, 4, 2, 2, 4
Y_ORDER = (4, 1, 7, 2, 6, 3, 5, 0)


def mm_nt(a, b):
    return lax.dot_general(a, b, (((1,), (1,)), ((), ())), preferred_element_type=jnp.float32)


def mm(a, b):
    return lax.dot_general(a, b, (((1,), (0,)), ((), ())), preferred_element_type=jnp.float32)


def split(v):
    hi = v.astype(jnp.bfloat16)
    return hi, (v - hi.astype(jnp.float32)).astype(jnp.bfloat16)


def kernel(ints, fit, occ, pat, out, r_int, r_fit, c_own, c_all, mask, th, tl, s_all, r_x, s_a, r_a, s_b, r_b,
           send_sem, int_sem, fit_sem, own_sem, all_sem, x_sem, a_sem, b_sem, send2_sem, sendx_sem, senda_sem, sendb_sem,
           ready):
    w = lax.axis_index("wide")
    n = lax.axis_index("narrow")
    y = w // (NZ * NC)
    zc = w % (NZ * NC)
    z = zc // NC
    c = zc % NC
    h = n // NX
    x = n % NX
    nw = NY * NZ * NC
    nq = ints.shape[0] // nw
    rows = ints.shape[1]
    basis = ints.shape[2]
    lanes = c_own.shape[2]

    def wide_id(yy, zz, cc):
        return (yy * NZ + zz) * NC + cc

    def beside(direction, core):
        if direction < 2:
            return {"wide": wide_id(lax.rem(y + (1, NY - 1)[direction], NY), z, core), "narrow": n}
        if direction < 4:
            zz = lax.rem(h * NZ + z + (1, NZ * NH - 1)[direction - 2], NZ * NH)
            return {"wide": wide_id(y, zz % NZ, core), "narrow": (zz // NZ) * NX + x}
        return {"wide": w + core - c, "narrow": h * NX + lax.rem(x + (1, NX - 1)[direction - 4], NX)}

    barrier = pltpu.get_barrier_semaphore()
    pl.semaphore_signal(barrier, inc=1, device_id={"wide": wide_id(y, z, 1 - c), "narrow": n})
    for direction in range(6):
        for core in range(NC):
            pl.semaphore_signal(barrier, inc=1, device_id=beside(direction, core))

    lane = lax.broadcasted_iota(jnp.int32, (1, basis), 1) // (basis // NBLK)
    for a in range(NBLK):
        v = jnp.zeros((1, basis), jnp.float32)
        for b in range(NBLK):
            v = jnp.where(lane == b, pat[a, b].astype(jnp.float32), v)
        mask[pl.ds(a * (basis // NBLK), basis // NBLK), :] = jnp.broadcast_to(
            v, (basis // NBLK, basis)).astype(jnp.bfloat16)

    pl.semaphore_wait(barrier, 1 + 6 * NC)

    def panel_copy(p, k):
        return pltpu.make_async_remote_copy(
            src_ref=occ.at[:, pl.ds(pl.multiple_of(k * lanes, lanes), lanes)], dst_ref=c_own.at[w],
            send_sem=send2_sem, recv_sem=own_sem, device_id={"wide": p, "narrow": n})

    def row_copy(src, dst, sem, p):
        return pltpu.make_async_remote_copy(
            src_ref=src.at[pl.ds(p * nq, nq)], dst_ref=dst.at[:, w],
            send_sem=send_sem, recv_sem=sem, device_id={"wide": p, "narrow": n})

    def first(p, core):
        panel_copy(p, x * NC + core).start()
        row_copy(ints, r_int, int_sem, p).start()

    first(wide_id(y, z, 1 - c), 1 - c)
    far = NY // 2 + NZ - 1
    for d in range(1, far + 1):
        if d > 1:
            for direction in range(6):
                pl.semaphore_signal(ready.at[(d - 2) * 6 + (direction ^ 1)], inc=1, device_id=beside(direction, c))
            for direction in range(6):
                pl.semaphore_wait(ready.at[(d - 2) * 6 + direction], 1)
        for dz in range(1 - NZ, NZ):
            steps = [dy for dy in range(NY) if min(dy, NY - dy) + abs(dz) == d]
            if steps:
                @pl.when(jnp.logical_and(z + dz >= 0, z + dz < NZ))
                def _():
                    for dy in steps:
                        for core in range(NC):
                            first(wide_id(lax.rem(y + dy, NY), z + dz, core), core)
    pltpu.make_async_copy(occ.at[:, pl.ds(pl.multiple_of((x * NC + c) * lanes, lanes), lanes)], c_own.at[w], own_sem).start()
    pltpu.make_async_copy(ints.at[pl.ds(w * nq, nq)], r_int.at[:, w], int_sem).start()

    for dy in Y_ORDER:
        base = lax.rem(y + dy, NY) * (NZ * NC)

        def step(o, carry):
            row_copy(fit, r_fit, fit_sem, base + (zc ^ o)).start()
            return carry

        lax.fori_loop(1 if dy == 0 else 0, NZ * NC, step, 0)
    pltpu.make_async_copy(fit.at[pl.ds(w * nq, nq)], r_fit.at[:, w], fit_sem).start()

    pltpu.make_async_copy(c_own, c_own, own_sem).wait()
    k_own = x * NC + c

    def pass_on(dx, dc):
        return pltpu.make_async_remote_copy(
            src_ref=c_own, dst_ref=c_all.at[k_own], send_sem=send2_sem, recv_sem=all_sem,
            device_id={"wide": wide_id(y, z, c ^ dc), "narrow": h * NX + lax.rem(x + dx, NX)})

    others = [(dx, dc) for dx in range(NX) for dc in range(NC) if (dx, dc) != (0, 0)]
    for dx, dc in others:
        pass_on(dx, dc).start()
    pltpu.make_async_copy(c_own, c_all.at[k_own], all_sem).start()
    pltpu.make_async_copy(c_all, c_all, all_sem).wait()
    panel = jnp.concatenate([c_all[k].reshape(basis, lanes) for k in range(NX * NC)], axis=1)
    p_hi, p_lo = split(mm_nt(panel, panel))

    pltpu.make_async_copy(r_int, r_int, int_sem).wait()
    keep = mask[...]
    for q in range(nq):
        a = r_int[q].reshape(basis, basis) * keep
        hi, lo = split(mm(a, p_hi) + mm(a, p_lo))
        th[q] = hi
        tl[q] = lo

    pltpu.make_async_copy(r_fit, r_fit, fit_sem).wait()
    m = jnp.zeros((basis, basis), jnp.float32)
    for q in range(nq):
        f = r_fit[q].reshape(basis, basis) * keep
        m = m + mm_nt(th[q], f) + mm_nt(tl[q], f)
    s = (m + m.T).reshape(NY * NZ, NC, rows, basis)

    for core in range(NC):
        s_all[core] = s[:, core]
    swap = pltpu.make_async_remote_copy(
        src_ref=s_all.at[1 - c], dst_ref=r_x, send_sem=sendx_sem, recv_sem=x_sem,
        device_id={"wide": wide_id(y, z, 1 - c), "narrow": n})
    swap.start()
    swap.wait_recv()
    s_a[...] = (s_all[c] + r_x[...]).reshape(NY, NZ, rows, basis)

    def copy_a(dy):
        yy = lax.rem(y + dy, NY)
        return pltpu.make_async_remote_copy(
            src_ref=s_a.at[yy], dst_ref=r_a.at[y], send_sem=senda_sem, recv_sem=a_sem,
            device_id={"wide": wide_id(yy, z, c), "narrow": n})

    for dy in Y_ORDER:
        if dy:
            copy_a(dy).start()
    pltpu.make_async_copy(s_a.at[y], r_a.at[y], a_sem).start()
    pltpu.make_async_copy(r_a, r_a, a_sem).wait()
    s_b[...] = jnp.sum(r_a[...], axis=0)

    me_b = n * NZ + z

    def copy_b(j, dz):
        nn = lax.rem(n + j, NH * NX)
        zz = z ^ dz
        return pltpu.make_async_remote_copy(
            src_ref=s_b.at[zz], dst_ref=r_b.at[me_b], send_sem=sendb_sem, recv_sem=b_sem,
            device_id={"wide": wide_id(y, zz, c), "narrow": nn})

    for j in range(NH * NX):
        for dz in range(NZ):
            if (j, dz) != (0, 0):
                copy_b(j, dz).start()
    pltpu.make_async_copy(s_b.at[z], r_b.at[me_b], b_sem).start()
    pltpu.make_async_copy(r_b, r_b, b_sem).wait()
    out[...] = jnp.sum(r_b[...], axis=0)

    sent = ints.at[pl.ds(0, (nw - 1) * nq)]
    pltpu.make_async_copy(sent, sent, send_sem).wait()
    pltpu.make_async_copy(sent, sent, send_sem).wait()
    own = c_own.at[pl.ds(0, nw - 1)]
    pltpu.make_async_copy(own, own, send2_sem).wait()
    rest = c_all.at[pl.ds(0, NX * NC - 1)]
    pltpu.make_async_copy(rest, rest, send2_sem).wait()
    swap.wait_send()
    ra = r_a.at[pl.ds(0, NY - 1)]
    pltpu.make_async_copy(ra, ra, senda_sem).wait()
    rb = r_b.at[pl.ds(0, NH * NX * NZ - 1)]
    pltpu.make_async_copy(rb, rb, sendb_sem).wait()


def on_device(integrals, fitted, occupied, pattern):
    aux, rows, basis = integrals.shape
    width = occupied.shape[1]
    nw = NY * NZ * NC
    nq = aux // nw
    lanes = width // (NX * NC)
    bf, f32 = jnp.bfloat16, jnp.float32
    any_space = pl.BlockSpec(memory_space=pl.ANY)
    dma = pltpu.SemaphoreType.DMA
    return pl.pallas_call(
        kernel,
        out_shape=jax.ShapeDtypeStruct((rows, basis), f32),
        in_specs=[any_space, any_space, any_space, pl.BlockSpec(memory_space=pltpu.SMEM)],
        out_specs=pl.BlockSpec(memory_space=pltpu.VMEM),
        scratch_shapes=[
            pltpu.VMEM((nq, nw, rows, basis), bf),
            pltpu.VMEM((nq, nw, rows, basis), bf),
            pltpu.VMEM((nw, rows, lanes), bf),
            pltpu.VMEM((NX * NC, nw, rows, lanes), bf),
            pltpu.VMEM((basis, basis), bf),
            pltpu.VMEM((nq, basis, basis), bf),
            pltpu.VMEM((nq, basis, basis), bf),
            pltpu.VMEM((NC, NY * NZ, rows, basis), f32),
            pltpu.VMEM((NY * NZ, rows, basis), f32),
            pltpu.VMEM((NY, NZ, rows, basis), f32),
            pltpu.VMEM((NY, NZ, rows, basis), f32),
            pltpu.VMEM((NZ, rows, basis), f32),
            pltpu.VMEM((NH * NX * NZ, rows, basis), f32),
        ] + [dma] * 12 + [pltpu.SemaphoreType.REGULAR((6 * max(1, NY // 2 + NZ - 2),))],
        compiler_params=pltpu.CompilerParams(collective_id=0, has_side_effects=True),
    )(integrals, fitted, occupied, pattern)


def solution(mesh):
    in_specs = (P("narrow", "wide", None), P("narrow", "wide", None), P("wide", None), P())
    out_specs = P("wide", None)
    return jax.shard_map(
        on_device, mesh=mesh, in_specs=in_specs, out_specs=out_specs, check_vma=False
    )
```

```python
import functools

import jax
import jax.numpy as jnp
from jax import lax
from jax.experimental import pallas as pl
from jax.experimental.pallas import tpu as pltpu
from jax.sharding import PartitionSpec as P

NBLK = 8
NY, NZ, NC, NH, NX = 8, 4, 2, 2, 4
Y_ORDER = (4, 1, 7, 2, 6, 3, 5, 0)
Y_NEAR = (0, 1, 7, 2, 6, 3, 5, 4)
NEAR = 1


def mm_nt(a, b):
    return lax.dot_general(a, b, (((1,), (1,)), ((), ())), preferred_element_type=jnp.float32)


def mm(a, b):
    return lax.dot_general(a, b, (((1,), (0,)), ((), ())), preferred_element_type=jnp.float32)


def split(v):
    hi = v.astype(jnp.bfloat16)
    return hi, (v - hi.astype(jnp.float32)).astype(jnp.bfloat16)


def kernel(ints, fit, occ, pat, out, r_int, r_fit, c_own, c_all, mask, th, tl, s_all, r_x, s_a, r_a, s_b, r_b,
           send_sem, int_sem, fit_sem, own_sem, all_sem, x_sem, a_sem, b_sem, send2_sem, sendx_sem, senda_sem, sendb_sem,
           ready, cross):
    w = lax.axis_index("wide")
    n = lax.axis_index("narrow")
    y = w // (NZ * NC)
    zc = w % (NZ * NC)
    z = zc // NC
    c = zc % NC
    h = n // NX
    x = n % NX
    nw = NY * NZ * NC
    nq = ints.shape[0] // nw
    rows = ints.shape[1]
    basis = ints.shape[2]
    lanes = c_own.shape[2]

    def wide_id(yy, zz, cc):
        return (yy * NZ + zz) * NC + cc

    def along_x(dx):
        return {"wide": w, "narrow": h * NX + lax.rem(x + dx, NX)}

    def beside(direction, core):
        if direction < 2:
            return {"wide": wide_id(lax.rem(y + (1, NY - 1)[direction], NY), z, core), "narrow": n}
        return {"wide": wide_id(y, z + (1, -1)[direction - 2], core), "narrow": n}

    def four(do):
        do(0)
        do(1)

        @pl.when(z < NZ - 1)
        def _():
            do(2)

        @pl.when(z > 0)
        def _():
            do(3)

    barrier = pltpu.get_barrier_semaphore()
    pl.semaphore_signal(barrier, inc=1, device_id={"wide": wide_id(y, z, 1 - c), "narrow": n})

    def greet(direction):
        for core in range(NC):
            pl.semaphore_signal(barrier, inc=1, device_id=beside(direction, core))

    four(greet)
    for dx in (1, NX - 1):
        pl.semaphore_signal(barrier, inc=1, device_id=along_x(dx))
    edge = jnp.logical_or(jnp.logical_and(h == 0, z == NZ - 1), jnp.logical_and(h == 1, z == 0))
    over = {"wide": wide_id(y, NZ - 1 - z, c), "narrow": (1 - h) * NX + x}

    @pl.when(edge)
    def _():
        pl.semaphore_signal(barrier, inc=1, device_id=over)

    lane = lax.broadcasted_iota(jnp.int32, (1, basis), 1) // (basis // NBLK)
    for a in range(NBLK):
        v = jnp.zeros((1, basis), jnp.float32)
        for b in range(NBLK):
            v = jnp.where(lane == b, pat[a, b].astype(jnp.float32), v)
        mask[pl.ds(a * (basis // NBLK), basis // NBLK), :] = jnp.broadcast_to(
            v, (basis // NBLK, basis)).astype(jnp.bfloat16)

    inner = (z < NZ - 1).astype(jnp.int32) + (z > 0).astype(jnp.int32)
    pl.semaphore_wait(barrier, 1 + NC * (2 + inner) + 2 + edge.astype(jnp.int32))
    rounds = NY // 2 + NZ - 2

    def panel_copy(p, k, dy):
        return pltpu.make_async_remote_copy(
            src_ref=occ.at[:, pl.ds(pl.multiple_of(k * lanes, lanes), lanes)], dst_ref=c_own.at[w],
            send_sem=send2_sem, recv_sem=own_sem.at[(NY - dy) % NY], device_id={"wide": p, "narrow": n})

    def row_copy(src, dst, sem, p):
        return pltpu.make_async_remote_copy(
            src_ref=src.at[pl.ds(p * nq, nq)], dst_ref=dst.at[:, w],
            send_sem=send_sem, recv_sem=sem, device_id={"wide": p, "narrow": n})

    def targets(d, do):
        for dz in range(1 - NZ, NZ):
            steps = [dy for dy in range(NY) if min(dy, NY - dy) + abs(dz) == d]
            if steps:
                @pl.when(jnp.logical_and(z + dz >= 0, z + dz < NZ))
                def _():
                    for dy in steps:
                        for core in range(NC):
                            do(wide_id(lax.rem(y + dy, NY), z + dz, core), core, dy)

    def send_fit(p, core, dy):
        row_copy(fit, r_fit, fit_sem, p).start()

    def send(p, core, dy):
        panel_copy(p, x * NC + core, dy).start()
        row_copy(ints, r_int, int_sem, p).start()

    send(wide_id(y, z, 1 - c), 1 - c, 0)
    send_fit(wide_id(y, z, 1 - c), 1 - c, 0)
    for d in range(1, rounds + 2):
        if d > 1:
            four(lambda direction: pl.semaphore_signal(
                ready.at[(d - 2) * 4 + (direction ^ 1)], inc=1, device_id=beside(direction, c)))
            four(lambda direction: pl.semaphore_wait(ready.at[(d - 2) * 4 + direction], 1))
        targets(d, send)
        if d <= NEAR:
            targets(d, send_fit)
    for d in range(rounds + 1, NEAR, -1):
        targets(d, send_fit)
    pltpu.make_async_copy(occ.at[:, pl.ds(pl.multiple_of((x * NC + c) * lanes, lanes), lanes)], c_own.at[w], own_sem.at[0]).start()
    pltpu.make_async_copy(ints.at[pl.ds(w * nq, nq)], r_int.at[:, w], int_sem).start()
    pltpu.make_async_copy(fit.at[pl.ds(w * nq, nq)], r_fit.at[:, w], fit_sem).start()
    for dx in (1, NX - 1):
        pl.semaphore_signal(cross.at[0], inc=1, device_id=along_x(dx))

    pl.semaphore_wait(cross.at[0], 2)
    for dx in (1, NX - 1):
        pl.semaphore_signal(cross.at[1], inc=1, device_id=along_x(dx))
    pl.semaphore_wait(cross.at[1], 2)

    k_own = x * NC + c
    slab = NZ * NC
    others = [(dx, dc) for dx in range(NX) for dc in range(NC) if (dx, dc) != (0, 0)]
    for dy in Y_NEAR:
        here = pl.ds(lax.rem(y + dy, NY) * slab, slab)
        pltpu.make_async_copy(c_own.at[here], c_own.at[here], own_sem.at[dy]).wait()
        for dx, dc in others:
            pltpu.make_async_remote_copy(
                src_ref=c_own.at[here], dst_ref=c_all.at[k_own, here], send_sem=send2_sem, recv_sem=all_sem,
                device_id={"wide": wide_id(y, z, c ^ dc), "narrow": h * NX + lax.rem(x + dx, NX)}).start()
        pltpu.make_async_copy(c_own.at[here], c_all.at[k_own, here], all_sem).start()

    @pl.when(edge)
    def _():
        pl.semaphore_signal(cross.at[2], inc=1, device_id=over)
        pl.semaphore_wait(cross.at[2], 1)
        for dz in range(1, NZ):
            pl.semaphore_signal(cross.at[3], inc=1, device_id={"wide": wide_id(y, z ^ dz, c), "narrow": n})

    @pl.when(jnp.logical_not(edge))
    def _():
        pl.semaphore_wait(cross.at[3], 1)

    pltpu.make_async_copy(c_all, c_all, all_sem).wait()
    panel = jnp.concatenate([c_all[k].reshape(basis, lanes) for k in range(NX * NC)], axis=1)
    p_hi, p_lo = split(mm_nt(panel, panel))

    pltpu.make_async_copy(r_int, r_int, int_sem).wait()
    keep = mask[...]
    for q in range(nq):
        a = r_int[q].reshape(basis, basis) * keep
        hi, lo = split(mm(a, p_hi) + mm(a, p_lo))
        th[q] = hi
        tl[q] = lo

    pltpu.make_async_copy(r_fit, r_fit, fit_sem).wait()
    m = jnp.zeros((basis, basis), jnp.float32)
    for q in range(nq):
        f = r_fit[q].reshape(basis, basis) * keep
        m = m + mm_nt(th[q], f) + mm_nt(tl[q], f)
    s = (m + m.T).reshape(NY * NZ, NC, rows, basis)

    for core in range(NC):
        s_all[core] = s[:, core]
    swap = pltpu.make_async_remote_copy(
        src_ref=s_all.at[1 - c], dst_ref=r_x, send_sem=sendx_sem, recv_sem=x_sem,
        device_id={"wide": wide_id(y, z, 1 - c), "narrow": n})
    swap.start()
    swap.wait_recv()
    s_a[...] = (s_all[c] + r_x[...]).reshape(NY, NZ, rows, basis)

    def copy_a(dy):
        yy = lax.rem(y + dy, NY)
        return pltpu.make_async_remote_copy(
            src_ref=s_a.at[yy], dst_ref=r_a.at[y], send_sem=senda_sem, recv_sem=a_sem,
            device_id={"wide": wide_id(yy, z, c), "narrow": n})

    for dy in Y_ORDER:
        if dy:
            copy_a(dy).start()
    pltpu.make_async_copy(s_a.at[y], r_a.at[y], a_sem).start()
    pltpu.make_async_copy(r_a, r_a, a_sem).wait()
    s_b[...] = jnp.sum(r_a[...], axis=0)

    me_b = n * NZ + z

    def copy_b(j, dz):
        nn = lax.rem(n + j, NH * NX)
        zz = z ^ dz
        return pltpu.make_async_remote_copy(
            src_ref=s_b.at[zz], dst_ref=r_b.at[me_b], send_sem=sendb_sem, recv_sem=b_sem,
            device_id={"wide": wide_id(y, zz, c), "narrow": nn})

    for j in range(NH * NX):
        for dz in range(NZ):
            if (j, dz) != (0, 0):
                copy_b(j, dz).start()
    pltpu.make_async_copy(s_b.at[z], r_b.at[me_b], b_sem).start()
    pltpu.make_async_copy(r_b, r_b, b_sem).wait()
    out[...] = jnp.sum(r_b[...], axis=0)

    sent = ints.at[pl.ds(0, (nw - 1) * nq)]
    pltpu.make_async_copy(sent, sent, send_sem).wait()
    pltpu.make_async_copy(sent, sent, send_sem).wait()
    own = c_own.at[pl.ds(0, nw - 1)]
    pltpu.make_async_copy(own, own, send2_sem).wait()
    rest = c_all.at[pl.ds(0, NX * NC - 1)]
    pltpu.make_async_copy(rest, rest, send2_sem).wait()
    swap.wait_send()
    ra = r_a.at[pl.ds(0, NY - 1)]
    pltpu.make_async_copy(ra, ra, senda_sem).wait()
    rb = r_b.at[pl.ds(0, NH * NX * NZ - 1)]
    pltpu.make_async_copy(rb, rb, sendb_sem).wait()


def on_device(integrals, fitted, occupied, pattern):
    aux, rows, basis = integrals.shape
    width = occupied.shape[1]
    nw = NY * NZ * NC
    nq = aux // nw
    lanes = width // (NX * NC)
    bf, f32 = jnp.bfloat16, jnp.float32
    any_space = pl.BlockSpec(memory_space=pl.ANY)
    dma = pltpu.SemaphoreType.DMA
    return pl.pallas_call(
        kernel,
        out_shape=jax.ShapeDtypeStruct((rows, basis), f32),
        in_specs=[any_space, any_space, any_space, pl.BlockSpec(memory_space=pltpu.SMEM)],
        out_specs=pl.BlockSpec(memory_space=pltpu.VMEM),
        scratch_shapes=[
            pltpu.VMEM((nq, nw, rows, basis), bf),
            pltpu.VMEM((nq, nw, rows, basis), bf),
            pltpu.VMEM((nw, rows, lanes), bf),
            pltpu.VMEM((NX * NC, nw, rows, lanes), bf),
            pltpu.VMEM((basis, basis), bf),
            pltpu.VMEM((nq, basis, basis), bf),
            pltpu.VMEM((nq, basis, basis), bf),
            pltpu.VMEM((NC, NY * NZ, rows, basis), f32),
            pltpu.VMEM((NY * NZ, rows, basis), f32),
            pltpu.VMEM((NY, NZ, rows, basis), f32),
            pltpu.VMEM((NY, NZ, rows, basis), f32),
            pltpu.VMEM((NZ, rows, basis), f32),
            pltpu.VMEM((NH * NX * NZ, rows, basis), f32),
        ] + [dma] * 3 + [pltpu.SemaphoreType.DMA((NY,))] + [dma] * 8 + [
            pltpu.SemaphoreType.REGULAR((4 * max(1, NY // 2 + NZ - 2),)), pltpu.SemaphoreType.REGULAR((4,))],
        compiler_params=pltpu.CompilerParams(collective_id=0, has_side_effects=True),
    )(integrals, fitted, occupied, pattern)


def solution(mesh):
    in_specs = (P("narrow", "wide", None), P("narrow", "wide", None), P("wide", None), P())
    out_specs = P("wide", None)
    return jax.shard_map(
        on_device, mesh=mesh, in_specs=in_specs, out_specs=out_specs, check_vma=False
    )
```

```python
import functools

import jax
import jax.numpy as jnp
from jax import lax
from jax.experimental import pallas as pl
from jax.experimental.pallas import tpu as pltpu
from jax.sharding import PartitionSpec as P

NBLK = 8
NY, NZ, NC, NH, NX = 8, 4, 2, 2, 4
Y_ORDER = (4, 1, 7, 2, 6, 3, 5, 0)
Y_NEAR = (0, 1, 7, 2, 6, 3, 5, 4)
NEAR = 1


def mm_nt(a, b):
    return lax.dot_general(a, b, (((1,), (1,)), ((), ())), preferred_element_type=jnp.float32)


def mm(a, b):
    return lax.dot_general(a, b, (((1,), (0,)), ((), ())), preferred_element_type=jnp.float32)


def split(v):
    hi = v.astype(jnp.bfloat16)
    return hi, (v - hi.astype(jnp.float32)).astype(jnp.bfloat16)


def kernel(ints, fit, occ, pat, out, r_int, r_fit, c_own, c_all, mask, th, tl, s_all, r_x, s_a, r_a, s_b, r_b,
           send_sem, int_sem, fit_sem, own_sem, all_sem, x_sem, a_sem, b_sem, send2_sem, sendx_sem, senda_sem, sendb_sem,
           ready, cross):
    w = lax.axis_index("wide")
    n = lax.axis_index("narrow")
    y = w // (NZ * NC)
    zc = w % (NZ * NC)
    z = zc // NC
    c = zc % NC
    h = n // NX
    x = n % NX
    nw = NY * NZ * NC
    nq = ints.shape[0] // nw
    rows = ints.shape[1]
    basis = ints.shape[2]
    lanes = c_own.shape[2]

    def wide_id(yy, zz, cc):
        return (yy * NZ + zz) * NC + cc

    def along_x(dx):
        return {"wide": w, "narrow": h * NX + lax.rem(x + dx, NX)}

    def beside(direction, core):
        if direction < 2:
            return {"wide": wide_id(lax.rem(y + (1, NY - 1)[direction], NY), z, core), "narrow": n}
        return {"wide": wide_id(y, z + (1, -1)[direction - 2], core), "narrow": n}

    def four(do):
        do(0)
        do(1)

        @pl.when(z < NZ - 1)
        def _():
            do(2)

        @pl.when(z > 0)
        def _():
            do(3)

    barrier = pltpu.get_barrier_semaphore()
    pl.semaphore_signal(barrier, inc=1, device_id={"wide": wide_id(y, z, 1 - c), "narrow": n})

    def greet(direction):
        for core in range(NC):
            pl.semaphore_signal(barrier, inc=1, device_id=beside(direction, core))

    four(greet)
    for dx in (1, NX - 1):
        pl.semaphore_signal(barrier, inc=1, device_id=along_x(dx))
    edge = jnp.logical_or(jnp.logical_and(h == 0, z == NZ - 1), jnp.logical_and(h == 1, z == 0))
    over = {"wide": wide_id(y, NZ - 1 - z, c), "narrow": (1 - h) * NX + x}

    @pl.when(edge)
    def _():
        pl.semaphore_signal(barrier, inc=1, device_id=over)

    lane = lax.broadcasted_iota(jnp.int32, (1, basis), 1) // (basis // NBLK)
    for a in range(NBLK):
        v = jnp.zeros((1, basis), jnp.float32)
        for b in range(NBLK):
            v = jnp.where(lane == b, pat[a, b].astype(jnp.float32), v)
        mask[pl.ds(a * (basis // NBLK), basis // NBLK), :] = jnp.broadcast_to(
            v, (basis // NBLK, basis)).astype(jnp.bfloat16)

    inner = (z < NZ - 1).astype(jnp.int32) + (z > 0).astype(jnp.int32)
    pl.semaphore_wait(barrier, 1 + NC * (2 + inner) + 2 + edge.astype(jnp.int32))
    rounds = NY // 2 + NZ - 2

    def panel_copy(p, k, dy):
        return pltpu.make_async_remote_copy(
            src_ref=occ.at[:, pl.ds(pl.multiple_of(k * lanes, lanes), lanes)], dst_ref=c_own.at[w],
            send_sem=send2_sem, recv_sem=own_sem.at[(NY - dy) % NY], device_id={"wide": p, "narrow": n})

    def row_copy(src, dst, sem, p):
        return pltpu.make_async_remote_copy(
            src_ref=src.at[pl.ds(p * nq, nq)], dst_ref=dst.at[:, w],
            send_sem=send_sem, recv_sem=sem, device_id={"wide": p, "narrow": n})

    def targets(d, do):
        for dz in range(1 - NZ, NZ):
            steps = [dy for dy in range(NY) if min(dy, NY - dy) + abs(dz) == d]
            if steps:
                @pl.when(jnp.logical_and(z + dz >= 0, z + dz < NZ))
                def _():
                    for dy in steps:
                        for core in range(NC):
                            do(wide_id(lax.rem(y + dy, NY), z + dz, core), core, dy)

    def send_fit(p, core, dy):
        row_copy(fit, r_fit, fit_sem, p).start()

    def send(p, core, dy):
        panel_copy(p, x * NC + core, dy).start()
        row_copy(ints, r_int, int_sem, p).start()

    send(wide_id(y, z, 1 - c), 1 - c, 0)
    send_fit(wide_id(y, z, 1 - c), 1 - c, 0)
    for d in range(1, rounds + 2):
        if d > 1:
            four(lambda direction: pl.semaphore_signal(
                ready.at[(d - 2) * 4 + (direction ^ 1)], inc=1, device_id=beside(direction, c)))
            four(lambda direction: pl.semaphore_wait(ready.at[(d - 2) * 4 + direction], 1))
        targets(d, send)
        if d <= NEAR:
            targets(d, send_fit)
    for d in range(rounds + 1, NEAR, -1):
        targets(d, send_fit)
    pltpu.make_async_copy(occ.at[:, pl.ds(pl.multiple_of((x * NC + c) * lanes, lanes), lanes)], c_own.at[w], own_sem.at[0]).start()
    pltpu.make_async_copy(ints.at[pl.ds(w * nq, nq)], r_int.at[:, w], int_sem).start()
    pltpu.make_async_copy(fit.at[pl.ds(w * nq, nq)], r_fit.at[:, w], fit_sem).start()
    for dx in (1, NX - 1):
        pl.semaphore_signal(cross.at[0], inc=1, device_id=along_x(dx))

    pl.semaphore_wait(cross.at[0], 2)
    for dx in (1, NX - 1):
        pl.semaphore_signal(cross.at[1], inc=1, device_id=along_x(dx))
    pl.semaphore_wait(cross.at[1], 2)

    k_own = x * NC + c
    slab = NZ * NC
    others = [(dx, dc) for dx in range(NX) for dc in range(NC) if (dx, dc) != (0, 0)]
    for dy in Y_NEAR:
        here = pl.ds(lax.rem(y + dy, NY) * slab, slab)
        pltpu.make_async_copy(c_own.at[here], c_own.at[here], own_sem.at[dy]).wait()
        for dx, dc in others:
            pltpu.make_async_remote_copy(
                src_ref=c_own.at[here], dst_ref=c_all.at[k_own, here], send_sem=send2_sem, recv_sem=all_sem,
                device_id={"wide": wide_id(y, z, c ^ dc), "narrow": h * NX + lax.rem(x + dx, NX)}).start()
        pltpu.make_async_copy(c_own.at[here], c_all.at[k_own, here], all_sem).start()

    @pl.when(edge)
    def _():
        pl.semaphore_signal(cross.at[2], inc=1, device_id=over)
        pl.semaphore_wait(cross.at[2], 1)
        for dz in range(1, NZ):
            pl.semaphore_signal(cross.at[3], inc=1, device_id={"wide": wide_id(y, z ^ dz, c), "narrow": n})

    @pl.when(jnp.logical_not(edge))
    def _():
        pl.semaphore_wait(cross.at[3], 1)

    pltpu.make_async_copy(c_all, c_all, all_sem).wait()
    panel = jnp.concatenate([c_all[k].reshape(basis, lanes) for k in range(NX * NC)], axis=1)
    p_hi, p_lo = split(mm_nt(panel, panel))

    pltpu.make_async_copy(r_int, r_int, int_sem).wait()
    keep = mask[...]
    for q in range(nq):
        a = r_int[q].reshape(basis, basis) * keep
        hi, lo = split(mm(a, p_hi) + mm(a, p_lo))
        th[q] = hi
        tl[q] = lo

    pltpu.make_async_copy(r_fit, r_fit, fit_sem).wait()
    m = jnp.zeros((basis, basis), jnp.float32)
    for q in range(nq):
        f = r_fit[q].reshape(basis, basis) * keep
        m = m + mm_nt(th[q], f) + mm_nt(tl[q], f)
    s = (m + m.T).reshape(NY * NZ, NC, rows, basis)

    for core in range(NC):
        s_all[core] = s[:, core]
    swap = pltpu.make_async_remote_copy(
        src_ref=s_all.at[1 - c], dst_ref=r_x, send_sem=sendx_sem, recv_sem=x_sem,
        device_id={"wide": wide_id(y, z, 1 - c), "narrow": n})
    swap.start()
    swap.wait_recv()
    s_a[...] = (s_all[c] + r_x[...]).reshape(NY, NZ, rows, basis)

    def copy_a(dy):
        yy = lax.rem(y + dy, NY)
        return pltpu.make_async_remote_copy(
            src_ref=s_a.at[yy], dst_ref=r_a.at[y], send_sem=senda_sem, recv_sem=a_sem,
            device_id={"wide": wide_id(yy, z, c), "narrow": n})

    for dy in Y_ORDER:
        if dy:
            copy_a(dy).start()
    pltpu.make_async_copy(s_a.at[y], r_a.at[y], a_sem).start()
    pltpu.make_async_copy(r_a, r_a, a_sem).wait()
    s_b[...] = jnp.sum(r_a[...], axis=0)

    me_b = n * NZ + z

    def copy_b(j, dz):
        nn = lax.rem(n + j, NH * NX)
        zz = z ^ dz
        return pltpu.make_async_remote_copy(
            src_ref=s_b.at[zz], dst_ref=r_b.at[me_b], send_sem=sendb_sem, recv_sem=b_sem,
            device_id={"wide": wide_id(y, zz, c), "narrow": nn})

    for j in range(NH * NX):
        for dz in range(NZ):
            if (j, dz) != (0, 0):
                copy_b(j, dz).start()
    pltpu.make_async_copy(s_b.at[z], r_b.at[me_b], b_sem).start()
    pltpu.make_async_copy(r_b, r_b, b_sem).wait()
    out[...] = jnp.sum(r_b[...], axis=0)

    sent = ints.at[pl.ds(0, (nw - 1) * nq)]
    pltpu.make_async_copy(sent, sent, send_sem).wait()
    pltpu.make_async_copy(sent, sent, send_sem).wait()
    own = c_own.at[pl.ds(0, nw - 1)]
    pltpu.make_async_copy(own, own, send2_sem).wait()
    rest = c_all.at[pl.ds(0, NX * NC - 1)]
    pltpu.make_async_copy(rest, rest, send2_sem).wait()
    swap.wait_send()
    ra = r_a.at[pl.ds(0, NY - 1)]
    pltpu.make_async_copy(ra, ra, senda_sem).wait()
    rb = r_b.at[pl.ds(0, NH * NX * NZ - 1)]
    pltpu.make_async_copy(rb, rb, sendb_sem).wait()


def on_device(integrals, fitted, occupied, pattern):
    aux, rows, basis = integrals.shape
    width = occupied.shape[1]
    nw = NY * NZ * NC
    nq = aux // nw
    lanes = width // (NX * NC)
    bf, f32 = jnp.bfloat16, jnp.float32
    any_space = pl.BlockSpec(memory_space=pl.ANY)
    dma = pltpu.SemaphoreType.DMA
    return pl.pallas_call(
        kernel,
        out_shape=pltpu.VMEM((rows, basis), f32),
        in_specs=[any_space, any_space, any_space, pl.BlockSpec(memory_space=pltpu.SMEM)],
        out_specs=pl.BlockSpec(memory_space=pltpu.VMEM),
        scratch_shapes=[
            pltpu.VMEM((nq, nw, rows, basis), bf),
            pltpu.VMEM((nq, nw, rows, basis), bf),
            pltpu.VMEM((nw, rows, lanes), bf),
            pltpu.VMEM((NX * NC, nw, rows, lanes), bf),
            pltpu.VMEM((basis, basis), bf),
            pltpu.VMEM((nq, basis, basis), bf),
            pltpu.VMEM((nq, basis, basis), bf),
            pltpu.VMEM((NC, NY * NZ, rows, basis), f32),
            pltpu.VMEM((NY * NZ, rows, basis), f32),
            pltpu.VMEM((NY, NZ, rows, basis), f32),
            pltpu.VMEM((NY, NZ, rows, basis), f32),
            pltpu.VMEM((NZ, rows, basis), f32),
            pltpu.VMEM((NH * NX * NZ, rows, basis), f32),
        ] + [dma] * 3 + [pltpu.SemaphoreType.DMA((NY,))] + [dma] * 8 + [
            pltpu.SemaphoreType.REGULAR((4 * max(1, NY // 2 + NZ - 2),)), pltpu.SemaphoreType.REGULAR((4,))],
        compiler_params=pltpu.CompilerParams(collective_id=0, has_side_effects=True),
    )(integrals, fitted, occupied, pattern)


def solution(mesh):
    in_specs = (P("narrow", "wide", None), P("narrow", "wide", None), P("wide", None), P())
    out_specs = P("wide", None)
    return jax.shard_map(
        on_device, mesh=mesh, in_specs=in_specs, out_specs=out_specs, check_vma=False
    )
```

```python
import functools

import jax
import jax.numpy as jnp
from jax import lax
from jax.experimental import pallas as pl
from jax.experimental.pallas import tpu as pltpu
from jax.sharding import PartitionSpec as P

NBLK = 8
NY, NZ, NC, NH, NX = 8, 4, 2, 2, 4
Y_ORDER = (4, 1, 7, 2, 6, 3, 5, 0)
Y_NEAR = (0, 1, 7, 2, 6, 3, 5, 4)
NEAR = 1


def mm_nt(a, b):
    return lax.dot_general(a, b, (((1,), (1,)), ((), ())), preferred_element_type=jnp.float32)


def mm(a, b):
    return lax.dot_general(a, b, (((1,), (0,)), ((), ())), preferred_element_type=jnp.float32)


def split(v):
    hi = v.astype(jnp.bfloat16)
    return hi, (v - hi.astype(jnp.float32)).astype(jnp.bfloat16)


def kernel(ints, fit, occ, pat, out, r_int, r_fit, c_own, c_all, mask, th, tl, s_all, r_x, s_a, r_a, s_b, r_b,
           send_sem, int_sem, fit_sem, own_sem, all_sem, x_sem, a_sem, b_sem, send2_sem, sendx_sem, senda_sem, sendb_sem,
           ready, cross):
    w = lax.axis_index("wide")
    n = lax.axis_index("narrow")
    y = w // (NZ * NC)
    zc = w % (NZ * NC)
    z = zc // NC
    c = zc % NC
    h = n // NX
    x = n % NX
    nw = NY * NZ * NC
    nq = ints.shape[0] // nw
    rows = ints.shape[1]
    basis = ints.shape[2]
    lanes = c_own.shape[2]

    def wide_id(yy, zz, cc):
        return (yy * NZ + zz) * NC + cc

    def along_x(dx):
        return {"wide": w, "narrow": h * NX + lax.rem(x + dx, NX)}

    def beside(direction, core):
        if direction < 2:
            return {"wide": wide_id(lax.rem(y + (1, NY - 1)[direction], NY), z, core), "narrow": n}
        return {"wide": wide_id(y, z + (1, -1)[direction - 2], core), "narrow": n}

    def four(do):
        do(0)
        do(1)

        @pl.when(z < NZ - 1)
        def _():
            do(2)

        @pl.when(z > 0)
        def _():
            do(3)

    barrier = pltpu.get_barrier_semaphore()
    pl.semaphore_signal(barrier, inc=1, device_id={"wide": wide_id(y, z, 1 - c), "narrow": n})

    def greet(direction):
        for core in range(NC):
            pl.semaphore_signal(barrier, inc=1, device_id=beside(direction, core))

    four(greet)
    for dx in (1, NX - 1):
        pl.semaphore_signal(barrier, inc=1, device_id=along_x(dx))
    edge = jnp.logical_or(jnp.logical_and(h == 0, z == NZ - 1), jnp.logical_and(h == 1, z == 0))
    over = {"wide": wide_id(y, NZ - 1 - z, c), "narrow": (1 - h) * NX + x}

    @pl.when(edge)
    def _():
        pl.semaphore_signal(barrier, inc=1, device_id=over)

    lane = lax.broadcasted_iota(jnp.int32, (1, basis), 1) // (basis // NBLK)
    for a in range(NBLK):
        v = jnp.zeros((1, basis), jnp.float32)
        for b in range(NBLK):
            v = jnp.where(lane == b, pat[a, b].astype(jnp.float32), v)
        mask[pl.ds(a * (basis // NBLK), basis // NBLK), :] = jnp.broadcast_to(
            v, (basis // NBLK, basis)).astype(jnp.bfloat16)

    inner = (z < NZ - 1).astype(jnp.int32) + (z > 0).astype(jnp.int32)
    pl.semaphore_wait(barrier, 1 + NC * (2 + inner) + 2 + edge.astype(jnp.int32))
    rounds = NY // 2 + NZ - 2

    def panel_copy(p, k, dy):
        return pltpu.make_async_remote_copy(
            src_ref=occ.at[:, pl.ds(pl.multiple_of(k * lanes, lanes), lanes)], dst_ref=c_own.at[w],
            send_sem=send2_sem, recv_sem=own_sem.at[(NY - dy) % NY], device_id={"wide": p, "narrow": n})

    def row_copy(src, dst, sem, p):
        return pltpu.make_async_remote_copy(
            src_ref=src.at[pl.ds(p * nq, nq)], dst_ref=dst.at[:, w],
            send_sem=send_sem, recv_sem=sem, device_id={"wide": p, "narrow": n})

    def targets(d, do):
        for dz in range(1 - NZ, NZ):
            steps = [dy for dy in range(NY) if min(dy, NY - dy) + abs(dz) == d]
            if steps:
                @pl.when(jnp.logical_and(z + dz >= 0, z + dz < NZ))
                def _():
                    for dy in steps:
                        for core in range(NC):
                            do(wide_id(lax.rem(y + dy, NY), z + dz, core), core, dy)

    def send_fit(p, core, dy):
        row_copy(fit, r_fit, fit_sem, p).start()

    def send(p, core, dy):
        panel_copy(p, x * NC + core, dy).start()
        row_copy(ints, r_int, int_sem, p).start()

    send(wide_id(y, z, 1 - c), 1 - c, 0)
    send_fit(wide_id(y, z, 1 - c), 1 - c, 0)
    for d in range(1, rounds + 2):
        if d > 1:
            four(lambda direction: pl.semaphore_signal(
                ready.at[(d - 2) * 4 + (direction ^ 1)], inc=1, device_id=beside(direction, c)))
            four(lambda direction: pl.semaphore_wait(ready.at[(d - 2) * 4 + direction], 1))
        targets(d, send)
        if d <= NEAR:
            targets(d, send_fit)
    for d in range(rounds + 1, NEAR, -1):
        targets(d, send_fit)
    pltpu.make_async_copy(occ.at[:, pl.ds(pl.multiple_of((x * NC + c) * lanes, lanes), lanes)], c_own.at[w], own_sem.at[0]).start()
    pltpu.make_async_copy(ints.at[pl.ds(w * nq, nq)], r_int.at[:, w], int_sem).start()
    pltpu.make_async_copy(fit.at[pl.ds(w * nq, nq)], r_fit.at[:, w], fit_sem).start()
    for dx in (1, NX - 1):
        pl.semaphore_signal(cross.at[0], inc=1, device_id=along_x(dx))

    pl.semaphore_wait(cross.at[0], 2)
    for dx in (1, NX - 1):
        pl.semaphore_signal(cross.at[1], inc=1, device_id=along_x(dx))
    pl.semaphore_wait(cross.at[1], 2)

    k_own = x * NC + c
    slab = NZ * NC
    others = [(dx, dc) for dx in range(NX) for dc in range(NC) if (dx, dc) != (0, 0)]
    for dy in Y_NEAR:
        here = pl.ds(lax.rem(y + dy, NY) * slab, slab)
        pltpu.make_async_copy(c_own.at[here], c_own.at[here], own_sem.at[dy]).wait()
        for dx, dc in others:
            pltpu.make_async_remote_copy(
                src_ref=c_own.at[here], dst_ref=c_all.at[k_own, here], send_sem=send2_sem, recv_sem=all_sem,
                device_id={"wide": wide_id(y, z, c ^ dc), "narrow": h * NX + lax.rem(x + dx, NX)}).start()
        pltpu.make_async_copy(c_own.at[here], c_all.at[k_own, here], all_sem).start()

    @pl.when(edge)
    def _():
        pl.semaphore_signal(cross.at[2], inc=1, device_id=over)
        pl.semaphore_wait(cross.at[2], 1)
        for dz in range(1, NZ):
            pl.semaphore_signal(cross.at[3], inc=1, device_id={"wide": wide_id(y, z ^ dz, c), "narrow": n})

    @pl.when(jnp.logical_not(edge))
    def _():
        pl.semaphore_wait(cross.at[3], 1)

    pltpu.make_async_copy(c_all, c_all, all_sem).wait()
    panel = jnp.concatenate([c_all[k].reshape(basis, lanes) for k in range(NX * NC)], axis=1)
    p_hi, p_lo = split(mm_nt(panel, panel))

    pltpu.make_async_copy(r_int, r_int, int_sem).wait()
    keep = mask[...]
    for q in range(nq):
        a = r_int[q].reshape(basis, basis) * keep
        hi, lo = split(mm(a, p_hi) + mm(a, p_lo))
        th[q] = hi
        tl[q] = lo

    pltpu.make_async_copy(r_fit, r_fit, fit_sem).wait()
    m = jnp.zeros((basis, basis), jnp.float32)
    for q in range(nq):
        f = r_fit[q].reshape(basis, basis) * keep
        m = m + mm_nt(th[q], f) + mm_nt(tl[q], f)
    s = (m + m.T).reshape(NY * NZ, NC, rows, basis)

    for core in range(NC):
        s_all[core] = s[:, core]
    half = NY // 2 * NZ

    def swap(g):
        part = pl.ds(g * half, half)
        return pltpu.make_async_remote_copy(
            src_ref=s_all.at[1 - c, part], dst_ref=r_x.at[part], send_sem=sendx_sem.at[g], recv_sem=x_sem.at[g],
            device_id={"wide": wide_id(y, z, 1 - c), "narrow": n})

    swap(0).start()
    swap(1).start()

    for g in range(2):
        part = pl.ds(g * half, half)
        swap(g).wait_recv()
        s_a[pl.ds(g * (NY // 2), NY // 2)] = (s_all[c, part] + r_x[part]).reshape(NY // 2, NZ, rows, basis)
        for yy in range(g * (NY // 2), (g + 1) * (NY // 2)):
            @pl.when(y != yy)
            def _():
                pltpu.make_async_remote_copy(
                    src_ref=s_a.at[yy], dst_ref=r_a.at[y], send_sem=senda_sem, recv_sem=a_sem,
                    device_id={"wide": wide_id(yy, z, c), "narrow": n}).start()
    pltpu.make_async_copy(s_a.at[y], r_a.at[y], a_sem).start()
    pltpu.make_async_copy(r_a, r_a, a_sem).wait()
    s_b[...] = jnp.sum(r_a[...], axis=0)

    me_b = n * NZ + z

    def copy_b(j, dz):
        nn = lax.rem(n + j, NH * NX)
        zz = z ^ dz
        return pltpu.make_async_remote_copy(
            src_ref=s_b.at[zz], dst_ref=r_b.at[me_b], send_sem=sendb_sem, recv_sem=b_sem,
            device_id={"wide": wide_id(y, zz, c), "narrow": nn})

    for j in range(NH * NX):
        for dz in range(NZ):
            if (j, dz) != (0, 0):
                copy_b(j, dz).start()
    pltpu.make_async_copy(s_b.at[z], r_b.at[me_b], b_sem).start()
    pltpu.make_async_copy(r_b, r_b, b_sem).wait()
    out[...] = jnp.sum(r_b[...], axis=0)

    sent = ints.at[pl.ds(0, (nw - 1) * nq)]
    pltpu.make_async_copy(sent, sent, send_sem).wait()
    pltpu.make_async_copy(sent, sent, send_sem).wait()
    own = c_own.at[pl.ds(0, nw - 1)]
    pltpu.make_async_copy(own, own, send2_sem).wait()
    rest = c_all.at[pl.ds(0, NX * NC - 1)]
    pltpu.make_async_copy(rest, rest, send2_sem).wait()
    swap(0).wait_send()
    swap(1).wait_send()
    ra = r_a.at[pl.ds(0, NY - 1)]
    pltpu.make_async_copy(ra, ra, senda_sem).wait()
    rb = r_b.at[pl.ds(0, NH * NX * NZ - 1)]
    pltpu.make_async_copy(rb, rb, sendb_sem).wait()


def on_device(integrals, fitted, occupied, pattern):
    aux, rows, basis = integrals.shape
    width = occupied.shape[1]
    nw = NY * NZ * NC
    nq = aux // nw
    lanes = width // (NX * NC)
    bf, f32 = jnp.bfloat16, jnp.float32
    any_space = pl.BlockSpec(memory_space=pl.ANY)
    dma = pltpu.SemaphoreType.DMA
    return pl.pallas_call(
        kernel,
        out_shape=pltpu.VMEM((rows, basis), f32),
        in_specs=[any_space, any_space, any_space, pl.BlockSpec(memory_space=pltpu.SMEM)],
        out_specs=pl.BlockSpec(memory_space=pltpu.VMEM),
        scratch_shapes=[
            pltpu.VMEM((nq, nw, rows, basis), bf),
            pltpu.VMEM((nq, nw, rows, basis), bf),
            pltpu.VMEM((nw, rows, lanes), bf),
            pltpu.VMEM((NX * NC, nw, rows, lanes), bf),
            pltpu.VMEM((basis, basis), bf),
            pltpu.VMEM((nq, basis, basis), bf),
            pltpu.VMEM((nq, basis, basis), bf),
            pltpu.VMEM((NC, NY * NZ, rows, basis), f32),
            pltpu.VMEM((NY * NZ, rows, basis), f32),
            pltpu.VMEM((NY, NZ, rows, basis), f32),
            pltpu.VMEM((NY, NZ, rows, basis), f32),
            pltpu.VMEM((NZ, rows, basis), f32),
            pltpu.VMEM((NH * NX * NZ, rows, basis), f32),
        ] + [dma] * 3 + [dma((NY,)), dma] + [dma((2,))] + [dma] * 3 + [dma((2,))] + [dma] * 2 + [
            pltpu.SemaphoreType.REGULAR((4 * max(1, NY // 2 + NZ - 2),)), pltpu.SemaphoreType.REGULAR((4,))],
        compiler_params=pltpu.CompilerParams(collective_id=0, has_side_effects=True),
    )(integrals, fitted, occupied, pattern)


def solution(mesh):
    in_specs = (P("narrow", "wide", None), P("narrow", "wide", None), P("wide", None), P())
    out_specs = P("wide", None)
    return jax.shard_map(
        on_device, mesh=mesh, in_specs=in_specs, out_specs=out_specs, check_vma=False
    )
```

```python
import functools

import jax
import jax.numpy as jnp
from jax import lax
from jax.experimental import pallas as pl
from jax.experimental.pallas import tpu as pltpu
from jax.sharding import PartitionSpec as P

NBLK = 8
NY, NZ, NC, NH, NX = 8, 4, 2, 2, 4
Y_ORDER = (4, 1, 7, 2, 6, 3, 5, 0)
Y_NEAR = (0, 1, 7, 2, 6, 3, 5, 4)
NEAR = 1


def mm_nt(a, b):
    return lax.dot_general(a, b, (((1,), (1,)), ((), ())), preferred_element_type=jnp.float32)


def mm(a, b):
    return lax.dot_general(a, b, (((1,), (0,)), ((), ())), preferred_element_type=jnp.float32)


def split(v):
    hi = v.astype(jnp.bfloat16)
    return hi, (v - hi.astype(jnp.float32)).astype(jnp.bfloat16)


def kernel(ints, fit, occ, pat, out, r_int, r_fit, c_own, c_all, mask, th, tl, s_all, r_x, s_a, r_a, s_b, r_b,
           send_sem, int_sem, fit_sem, own_sem, all_sem, x_sem, a_sem, b_sem, send2_sem, sendx_sem, senda_sem, sendb_sem,
           ready, cross):
    w = lax.axis_index("wide")
    n = lax.axis_index("narrow")
    y = w // (NZ * NC)
    zc = w % (NZ * NC)
    z = zc // NC
    c = zc % NC
    h = n // NX
    x = n % NX
    nw = NY * NZ * NC
    nq = ints.shape[0] // nw
    rows = ints.shape[1]
    basis = ints.shape[2]
    lanes = c_own.shape[2]

    def wide_id(yy, zz, cc):
        return (yy * NZ + zz) * NC + cc

    def along_x(dx):
        return {"wide": w, "narrow": h * NX + lax.rem(x + dx, NX)}

    def beside(direction, core):
        if direction < 2:
            return {"wide": wide_id(lax.rem(y + (1, NY - 1)[direction], NY), z, core), "narrow": n}
        return {"wide": wide_id(y, z + (1, -1)[direction - 2], core), "narrow": n}

    def four(do):
        do(0)
        do(1)

        @pl.when(z < NZ - 1)
        def _():
            do(2)

        @pl.when(z > 0)
        def _():
            do(3)

    barrier = pltpu.get_barrier_semaphore()
    pl.semaphore_signal(barrier, inc=1, device_id={"wide": wide_id(y, z, 1 - c), "narrow": n})

    def greet(direction):
        for core in range(NC):
            pl.semaphore_signal(barrier, inc=1, device_id=beside(direction, core))

    four(greet)
    for dx in (1, NX - 1):
        pl.semaphore_signal(barrier, inc=1, device_id=along_x(dx))
    edge = jnp.logical_or(jnp.logical_and(h == 0, z == NZ - 1), jnp.logical_and(h == 1, z == 0))
    over = {"wide": wide_id(y, NZ - 1 - z, c), "narrow": (1 - h) * NX + x}

    @pl.when(edge)
    def _():
        pl.semaphore_signal(barrier, inc=1, device_id=over)

    inner = (z < NZ - 1).astype(jnp.int32) + (z > 0).astype(jnp.int32)
    pl.semaphore_wait(barrier, 1 + NC * (2 + inner) + 2 + edge.astype(jnp.int32))
    rounds = NY // 2 + NZ - 2

    def panel_copy(p, k, dy):
        return pltpu.make_async_remote_copy(
            src_ref=occ.at[:, pl.ds(pl.multiple_of(k * lanes, lanes), lanes)], dst_ref=c_own.at[w],
            send_sem=send2_sem, recv_sem=own_sem.at[(NY - dy) % NY], device_id={"wide": p, "narrow": n})

    def row_copy(src, dst, sem, p):
        return pltpu.make_async_remote_copy(
            src_ref=src.at[pl.ds(p * nq, nq)], dst_ref=dst.at[:, w],
            send_sem=send_sem, recv_sem=sem, device_id={"wide": p, "narrow": n})

    def targets(d, do):
        for dz in range(1 - NZ, NZ):
            steps = [dy for dy in range(NY) if min(dy, NY - dy) + abs(dz) == d]
            if steps:
                @pl.when(jnp.logical_and(z + dz >= 0, z + dz < NZ))
                def _():
                    for dy in steps:
                        for core in range(NC):
                            do(wide_id(lax.rem(y + dy, NY), z + dz, core), core, dy)

    def send_fit(p, core, dy):
        row_copy(fit, r_fit, fit_sem, p).start()

    def send(p, core, dy):
        panel_copy(p, x * NC + core, dy).start()
        row_copy(ints, r_int, int_sem, p).start()

    send(wide_id(y, z, 1 - c), 1 - c, 0)
    send_fit(wide_id(y, z, 1 - c), 1 - c, 0)
    for d in range(1, rounds + 2):
        if d > 1:
            four(lambda direction: pl.semaphore_signal(
                ready.at[(d - 2) * 4 + (direction ^ 1)], inc=1, device_id=beside(direction, c)))
            four(lambda direction: pl.semaphore_wait(ready.at[(d - 2) * 4 + direction], 1))
        targets(d, send)
        if d <= NEAR:
            targets(d, send_fit)
    for d in range(rounds + 1, NEAR, -1):
        targets(d, send_fit)
    pltpu.make_async_copy(occ.at[:, pl.ds(pl.multiple_of((x * NC + c) * lanes, lanes), lanes)], c_own.at[w], own_sem.at[0]).start()
    pltpu.make_async_copy(ints.at[pl.ds(w * nq, nq)], r_int.at[:, w], int_sem).start()
    pltpu.make_async_copy(fit.at[pl.ds(w * nq, nq)], r_fit.at[:, w], fit_sem).start()
    for dx in (1, NX - 1):
        pl.semaphore_signal(cross.at[0], inc=1, device_id=along_x(dx))

    pl.semaphore_wait(cross.at[0], 2)
    for dx in (1, NX - 1):
        pl.semaphore_signal(cross.at[1], inc=1, device_id=along_x(dx))
    pl.semaphore_wait(cross.at[1], 2)

    k_own = x * NC + c
    slab = NZ * NC
    others = [(dx, dc) for dx in range(NX) for dc in range(NC) if (dx, dc) != (0, 0)]
    for dy in Y_NEAR:
        here = pl.ds(lax.rem(y + dy, NY) * slab, slab)
        pltpu.make_async_copy(c_own.at[here], c_own.at[here], own_sem.at[dy]).wait()
        for dx, dc in others:
            pltpu.make_async_remote_copy(
                src_ref=c_own.at[here], dst_ref=c_all.at[k_own, here], send_sem=send2_sem, recv_sem=all_sem,
                device_id={"wide": wide_id(y, z, c ^ dc), "narrow": h * NX + lax.rem(x + dx, NX)}).start()
        pltpu.make_async_copy(c_own.at[here], c_all.at[k_own, here], all_sem).start()

    @pl.when(edge)
    def _():
        pl.semaphore_signal(cross.at[2], inc=1, device_id=over)
        pl.semaphore_wait(cross.at[2], 1)
        for dz in range(1, NZ):
            pl.semaphore_signal(cross.at[3], inc=1, device_id={"wide": wide_id(y, z ^ dz, c), "narrow": n})

    @pl.when(jnp.logical_not(edge))
    def _():
        pl.semaphore_wait(cross.at[3], 1)

    lane = lax.broadcasted_iota(jnp.int32, (1, basis), 1) // (basis // NBLK)
    for a in range(NBLK):
        v = jnp.zeros((1, basis), jnp.float32)
        for b in range(NBLK):
            v = jnp.where(lane == b, pat[a, b].astype(jnp.float32), v)
        mask[pl.ds(a * (basis // NBLK), basis // NBLK), :] = jnp.broadcast_to(
            v, (basis // NBLK, basis)).astype(jnp.bfloat16)

    pltpu.make_async_copy(c_all, c_all, all_sem).wait()
    panel = jnp.concatenate([c_all[k].reshape(basis, lanes) for k in range(NX * NC)], axis=1)
    p_hi, p_lo = split(mm_nt(panel, panel))

    pltpu.make_async_copy(r_int, r_int, int_sem).wait()
    keep = mask[...]
    for q in range(nq):
        a = r_int[q].reshape(basis, basis) * keep
        hi, lo = split(mm(a, p_hi) + mm(a, p_lo))
        th[q] = hi
        tl[q] = lo

    pltpu.make_async_copy(r_fit, r_fit, fit_sem).wait()
    m = jnp.zeros((basis, basis), jnp.float32)
    for q in range(nq):
        f = r_fit[q].reshape(basis, basis) * keep
        m = m + mm_nt(th[q], f) + mm_nt(tl[q], f)
    s = (m + m.T).reshape(NY * NZ, NC, rows, basis)

    for core in range(NC):
        s_all[core] = s[:, core]
    half = NY // 2 * NZ

    def swap(g):
        part = pl.ds(g * half, half)
        return pltpu.make_async_remote_copy(
            src_ref=s_all.at[1 - c, part], dst_ref=r_x.at[part], send_sem=sendx_sem.at[g], recv_sem=x_sem.at[g],
            device_id={"wide": wide_id(y, z, 1 - c), "narrow": n})

    swap(0).start()
    swap(1).start()

    for g in range(2):
        part = pl.ds(g * half, half)
        swap(g).wait_recv()
        s_a[pl.ds(g * (NY // 2), NY // 2)] = (s_all[c, part] + r_x[part]).reshape(NY // 2, NZ, rows, basis)
        for yy in range(g * (NY // 2), (g + 1) * (NY // 2)):
            @pl.when(y != yy)
            def _():
                pltpu.make_async_remote_copy(
                    src_ref=s_a.at[yy], dst_ref=r_a.at[y], send_sem=senda_sem, recv_sem=a_sem,
                    device_id={"wide": wide_id(yy, z, c), "narrow": n}).start()
    pltpu.make_async_copy(s_a.at[y], r_a.at[y], a_sem).start()
    pltpu.make_async_copy(r_a, r_a, a_sem).wait()
    s_b[...] = jnp.sum(r_a[...], axis=0)

    me_b = n * NZ + z

    def copy_b(j, dz):
        nn = lax.rem(n + j, NH * NX)
        zz = z ^ dz
        return pltpu.make_async_remote_copy(
            src_ref=s_b.at[zz], dst_ref=r_b.at[me_b], send_sem=sendb_sem, recv_sem=b_sem,
            device_id={"wide": wide_id(y, zz, c), "narrow": nn})

    for j in range(NH * NX):
        for dz in range(NZ):
            if (j, dz) != (0, 0):
                copy_b(j, dz).start()
    pltpu.make_async_copy(s_b.at[z], r_b.at[me_b], b_sem).start()
    pltpu.make_async_copy(r_b, r_b, b_sem).wait()
    out[...] = jnp.sum(r_b[...], axis=0)

    sent = ints.at[pl.ds(0, (nw - 1) * nq)]
    pltpu.make_async_copy(sent, sent, send_sem).wait()
    pltpu.make_async_copy(sent, sent, send_sem).wait()
    own = c_own.at[pl.ds(0, nw - 1)]
    pltpu.make_async_copy(own, own, send2_sem).wait()
    rest = c_all.at[pl.ds(0, NX * NC - 1)]
    pltpu.make_async_copy(rest, rest, send2_sem).wait()
    swap(0).wait_send()
    swap(1).wait_send()
    ra = r_a.at[pl.ds(0, NY - 1)]
    pltpu.make_async_copy(ra, ra, senda_sem).wait()
    rb = r_b.at[pl.ds(0, NH * NX * NZ - 1)]
    pltpu.make_async_copy(rb, rb, sendb_sem).wait()


def on_device(integrals, fitted, occupied, pattern):
    aux, rows, basis = integrals.shape
    width = occupied.shape[1]
    nw = NY * NZ * NC
    nq = aux // nw
    lanes = width // (NX * NC)
    bf, f32 = jnp.bfloat16, jnp.float32
    any_space = pl.BlockSpec(memory_space=pl.ANY)
    dma = pltpu.SemaphoreType.DMA
    return pl.pallas_call(
        kernel,
        out_shape=pltpu.VMEM((rows, basis), f32),
        in_specs=[any_space, any_space, any_space, pl.BlockSpec(memory_space=pltpu.SMEM)],
        out_specs=pl.BlockSpec(memory_space=pltpu.VMEM),
        scratch_shapes=[
            pltpu.VMEM((nq, nw, rows, basis), bf),
            pltpu.VMEM((nq, nw, rows, basis), bf),
            pltpu.VMEM((nw, rows, lanes), bf),
            pltpu.VMEM((NX * NC, nw, rows, lanes), bf),
            pltpu.VMEM((basis, basis), bf),
            pltpu.VMEM((nq, basis, basis), bf),
            pltpu.VMEM((nq, basis, basis), bf),
            pltpu.VMEM((NC, NY * NZ, rows, basis), f32),
            pltpu.VMEM((NY * NZ, rows, basis), f32),
            pltpu.VMEM((NY, NZ, rows, basis), f32),
            pltpu.VMEM((NY, NZ, rows, basis), f32),
            pltpu.VMEM((NZ, rows, basis), f32),
            pltpu.VMEM((NH * NX * NZ, rows, basis), f32),
        ] + [dma] * 3 + [dma((NY,)), dma] + [dma((2,))] + [dma] * 3 + [dma((2,))] + [dma] * 2 + [
            pltpu.SemaphoreType.REGULAR((4 * max(1, NY // 2 + NZ - 2),)), pltpu.SemaphoreType.REGULAR((4,))],
        compiler_params=pltpu.CompilerParams(collective_id=0, has_side_effects=True),
    )(integrals, fitted, occupied, pattern)


def solution(mesh):
    in_specs = (P("narrow", "wide", None), P("narrow", "wide", None), P("wide", None), P())
    out_specs = P("wide", None)
    return jax.shard_map(
        on_device, mesh=mesh, in_specs=in_specs, out_specs=out_specs, check_vma=False
    )
```
